32 devices in a mesh: sc: 4 (over y, x), rows: 8 (over z, core).
Axes of the slice: x: 2, y: 2, z: 4, core: 2. Of those that a mesh axis runs over, the one named last changes fastest.
Arguments:
- embeddings: bfloat16 [32768, 1024], P(('sc', 'rows')), may hold values from -6 to 6
- labels: int32 [32768, 1], P(('sc', 'rows')), may hold values from 0 to 3; in each aligned block of 1024 rows (0 to 1023, 1024 to 2047, ...) at most 512 rows name the same one
- init_idx: int32 [4, 256], P('sc'), may hold values from 0 to 16383
Outputs:
- assign: bfloat16 [32768, 256], P(('sc', 'rows'))
- centroids: float32 [4, 256, 1024], P('sc')
The draws below stay inside these ranges and needn't reach their ends.
Inputs may be any that keep to these rules, and one draw needn't show every extreme that they name: `labels`: among the rows of one device (aligned blocks of 1024 rows) no label occurs more than 512 times, and some label occurs exactly 512 times; every label occurs somewhere.
All inputs are finite; a program needn't handle non-finite values.
Results may differ from the reference program's by a relative error of at most 0.0052.
Values may be sent and summed in bfloat16 or wider, within the bound.
A program may use at most 64 MiB of HBM per device.

```python
import math
import jax
import jax.numpy as jnp
import numpy as np
from jax import lax

E = 1024
K = 256
TOK_DEV = 1024
ITERS = 3
ROUNDS = 3
SUPER = 4
CAP = 512
ROWS_ALL = 32768
DEVICES = 32


def draw_embeddings(key, part):
    centre_key = jax.random.fold_in(key, 101)
    block_key = jax.random.fold_in(key, 202)
    pick_key = jax.random.fold_in(key, 303)
    noise_key = jax.random.fold_in(key, 404)
    centre_count = 96
    block_count = ROWS_ALL // TOK_DEV
    centres = jax.random.normal(centre_key, (centre_count, E), jnp.float32)
    block_dirs = jax.random.normal(block_key, (block_count, E), jnp.float32)
    pick = jax.random.randint(pick_key, (ROWS_ALL,), 0, centre_count)
    block_of = jnp.arange(ROWS_ALL, dtype=jnp.int32) // TOK_DEV
    noise = jax.random.normal(noise_key, (ROWS_ALL, E), jnp.float32)
    values = centres[pick] + 0.8 * block_dirs[block_of] + 0.4 * noise
    return jnp.clip(values, -6.0, 6.0).astype(jnp.bfloat16)


def set_ends(drawn, key, low, top_value):
    dims = drawn.shape
    index_at = [jax.random.randint(jax.random.fold_in(key, axis), (), 0, dims[axis]) for axis in range(len(dims))]
    drawn = drawn.at[tuple(index_at)].set(low)
    longest = dims.index(max(dims))
    index_at[longest] = (index_at[longest] + 1) % dims[longest]
    return drawn.at[tuple(index_at)].set(top_value)


def shared_out(own_key, own, number, rows, count, top, reach, slope):
    order = jax.random.permutation(own_key, count)
    heavy_load, usual = load_shares(count, rows * top, reach, slope, True), load_shares(count, rows * top, reach, slope, False)
    places = jnp.arange(count)

    def named(sizes, offset_by):
        used = int((sizes > 0).sum())
        fixed = max(1, used // 4)
        shifted = fixed + (places - fixed + offset_by * (used - fixed)) % max(1, count - fixed)
        return jnp.zeros((count,), jnp.int32).at[order[jnp.where(places < fixed, places, shifted)]].set(jnp.asarray(sizes, jnp.int32))

    sizes = jnp.where(number % 4 == 0, named(heavy_load, number // 4), named(usual, number - number // 4 - 1))
    mixed = jax.random.permutation(jax.random.fold_in(own, 3), count)
    donor, taker = mixed[0:count // 2 * 2:2], mixed[1:count // 2 * 2:2]
    slack = jnp.minimum(sizes[donor] - 1, reach - sizes[taker]) // 2
    slack = jnp.where((donor == order[0]) | (taker == order[0]) | (sizes[taker] == 0), 0, jnp.maximum(slack, 0))
    shifted = jax.random.randint(jax.random.fold_in(own, 4), (count // 2,), 0, 1 << 20) % (slack + 1)
    sizes = sizes.at[donor].add(-shifted).at[taker].add(shifted)
    items = jnp.searchsorted(jnp.cumsum(sizes), jnp.arange(rows * top), side="right").astype(jnp.int32)
    listing = items.reshape(top, rows).T
    listing = listing[jax.random.permutation(jax.random.fold_in(own, 1), rows)]
    offset_by = jax.random.randint(jax.random.fold_in(own, 2), (rows, 1), 0, top)
    return jnp.take_along_axis(listing, (jnp.arange(top)[None, :] + offset_by) % top, axis=1)


def load_shares(amount, total, limit, slope, full):
    weights = [(1 << 20) // math.isqrt(grade ** slope) + 1 for grade in range(1, amount + 1)]
    largest = limit if full else min(limit, max(-(-total // amount), total * weights[0] // sum(weights)))
    least = 1 if total - largest >= amount - 1 else 0
    holding, surplus = [largest] + [least] * (amount - 1), total - largest - least * (amount - 1)
    while surplus > 0:
        candidates = [i for i in range(1, amount) if holding[i] < largest] or [i for i in range(1, amount) if holding[i] < limit]
        whole, remaining = sum([weights[i] for i in candidates]), surplus
        for i in candidates:
            addition = min(limit - holding[i], max(1, remaining * weights[i] // whole), surplus)
            holding[i] = holding[i] + addition
            surplus = surplus - addition
    return np.array(holding)


def setup_inputs(seed: int = 0) -> dict:
    seeds = jax.random.split(jax.random.key(seed), 4)
    embeddings = draw_embeddings(jax.random.fold_in(seeds[3], 71), 0)
    labels_keys = jax.random.split(jax.random.fold_in(seeds[1], 1), ROWS_ALL // TOK_DEV)
    labels_turns = jax.random.permutation(jax.random.fold_in(seeds[1], 3), ROWS_ALL // TOK_DEV)
    labels = jax.vmap(lambda own, number: shared_out(jax.random.fold_in(seeds[1], 2), own, number, TOK_DEV, SUPER, 1, CAP, 2))(labels_keys, labels_turns).reshape((ROWS_ALL, 1))
    init_idx = set_ends(jax.random.randint(seeds[2], (SUPER, K), 0, DEVICES * CAP), jax.random.fold_in(seeds[2], 1), 0, (DEVICES * CAP) - 1).astype(jnp.int32)
    return {"embeddings": embeddings, "labels": labels, "init_idx": init_idx}


def unit_of(rows):
    values = rows.astype(jnp.float32)
    scale = lax.rsqrt(lax.optimization_barrier(jnp.mean(values * values, axis=1, keepdims=True)) + 1e-05) * (1.0 / math.sqrt(rows.shape[1]))
    return (values * scale).astype(jnp.bfloat16)

def balance(plan, valid):
    for step in range(ITERS):
        plan = plan / lax.optimization_barrier(jnp.sum(plan, axis=0))[None, :]
        row_sum = lax.optimization_barrier(jnp.sum(plan, axis=1))
        plan = jnp.where(valid[:, None], plan / jnp.where(valid, row_sum, 1.0)[:, None], 0.0)
    return plan

def run_rounds(members, valid, cent):
    for round_index in range(ROUNDS):
        scores = jnp.dot(members, cent.T, preferred_element_type=jnp.float32)
        plan = jnp.where(valid[:, None], jnp.exp(scores * 10.0), 0.0)
        plan = balance(plan, valid)
        plan_b = plan.astype(jnp.bfloat16)
        mass = jnp.dot(plan_b.T, members, preferred_element_type=jnp.float32)
        if round_index < ROUNDS - 1:
            cent = (mass * lax.rsqrt(lax.optimization_barrier(jnp.sum(mass * mass, axis=1, keepdims=True)) + 1e-06)).astype(jnp.bfloat16)
        else:
            means = mass / lax.optimization_barrier(jnp.sum(plan, axis=0))[:, None]
    return (means, plan)

def reference(embeddings, labels, init_idx):
    label_col = labels[:, 0]
    total_rows = label_col.shape[0]
    unit_rows = unit_of(embeddings)
    order = jnp.argsort(label_col, stable=True).astype(jnp.int32)
    member = (label_col[:, None] == jnp.arange(SUPER, dtype=jnp.int32)[None, :]).astype(jnp.int32)
    counts = lax.optimization_barrier(jnp.sum(member, axis=0))
    starts = jnp.cumsum(counts) - counts
    longest = DEVICES * CAP

    def one_group(assign, group):
        count = counts[group]
        offsets = jnp.arange(longest, dtype=jnp.int32)
        valid = offsets < count
        index = order[jnp.clip(starts[group] + offsets, 0, total_rows - 1)]
        members = jnp.where(valid[:, None], unit_rows[index], jnp.zeros_like(unit_rows[index]))
        wanted = init_idx[group] % count
        cent = members[wanted]
        means, plan = run_rounds(members, valid, cent)
        target = jnp.where(valid, index, total_rows)
        assign = assign.at[target].set(plan.astype(jnp.bfloat16), mode='drop')
        return (assign, means)
    start_assign = jnp.zeros((total_rows, K), jnp.bfloat16)
    assign, centroids = lax.scan(one_group, start_assign, jnp.arange(SUPER, dtype=jnp.int32))
    return (assign, centroids)
```

```python
import functools
import math

import jax
import jax.numpy as jnp
from jax import lax
from jax.experimental import pallas as pl
from jax.experimental.pallas import tpu as pltpu
from jax.sharding import PartitionSpec as P

ITERS = 3
ROUNDS = 3
MESH = pl.DeviceIdType.MESH
F32 = jnp.float32
BF16 = jnp.bfloat16


def kernel(
    G, R, tok, E, K, S, T,
    x_ref, labr_ref, labc_ref, init_ref,
    assign_ref, means_ref,
    xu, out, inc, plan, planb, lhst, acc, ret, target,
    cnt, cntr, cs, s1s, s1r, s2s, s2r, cent,
    d_ss, d_rs, c_ss, c_rs, k_ss, k_rs, cs_ss, cs_rs,
    s1_ss, s1_rs, s2_ss, s2_rs, g_ss, g_rs, f_ss, f_rs, r_ss, r_rs,
):
    g = lax.axis_index("sc")
    r = lax.axis_index("rows")
    Z = R // 2
    H = K // 2
    Q = H // Z
    N = G * S
    z = r // 2
    c = r % 2
    oc = 1 - c
    partner = z * 2 + oc

    def copy(src, dst, ss, rs, to):
        return pltpu.make_async_remote_copy(
            src_ref=src, dst_ref=dst, send_sem=ss, recv_sem=rs,
            device_id=to, device_id_type=MESH,
        )

    barrier = pltpu.get_barrier_semaphore()
    for off in range(1, R):
        pl.semaphore_signal(barrier, inc=1, device_id=(g, (r + off) % R), device_id_type=MESH)
    for off in range(1, G):
        pl.semaphore_signal(barrier, inc=1, device_id=((g + off) % G, r), device_id_type=MESH)

    def unit(i, carry):
        at = pl.ds(pl.multiple_of(i * 128, 128), 128)
        v = x_ref[at, :].astype(F32)
        scale = lax.rsqrt(jnp.mean(v * v, axis=1, keepdims=True) + 1e-05) * (1.0 / math.sqrt(E))
        xu[at, :] = (v * scale).astype(BF16)
        return carry

    lax.fori_loop(0, tok // 128, unit, 0)

    labr = labr_ref[...]
    labc = labc_ref[...]
    sub = lax.broadcasted_iota(jnp.int32, (tok, tok), 0)
    lane = lax.broadcasted_iota(jnp.int32, (tok, tok), 1)
    tri = jnp.where(sub < lane, 1.0, 0.0).astype(BF16)
    mem_r = jnp.where(lax.broadcasted_iota(jnp.int32, (16, tok), 0) == labr, 1.0, 0.0)
    before_r = jnp.dot(mem_r.astype(BF16), tri, preferred_element_type=F32)
    place_r = jnp.sum(before_r * mem_r, axis=0, keepdims=True)
    tri_l = jnp.where(sub > lane, 1.0, 0.0).astype(BF16)
    mem_c = jnp.where(lax.broadcasted_iota(jnp.int32, (tok, 128), 1) == labc, 1.0, 0.0)
    before_c = jnp.dot(tri_l, mem_c.astype(BF16), preferred_element_type=F32)
    place_c = jnp.sum(before_c * mem_c, axis=1, keepdims=True)
    target[...] = labc * S + place_c.astype(jnp.int32)
    place_i = place_r.astype(jnp.int32)
    cnt[g] = jnp.sum(mem_c, axis=0, keepdims=True)

    pl.semaphore_wait(barrier, R - 1 + G - 1)

    count_sends = []
    for off in range(1, G):
        to = (g + off) % G
        d = copy(cnt.at[g], cnt.at[g], c_ss.at[off], c_rs.at[g], (to, r))
        d.start()
        count_sends.append(d)

    DT = min(256, S)
    per = S // DT
    row_sends = []
    for off in range(1, G + 1):
        to = (g + off) % G
        chosen = jnp.where(labr == to, place_i, -1)
        for j in range(per):
            slot = lax.broadcasted_iota(jnp.int32, (DT, tok), 0) + j * DT
            perm = jnp.where(slot == chosen, 1.0, 0.0).astype(BF16)
            block = jnp.dot(perm, xu[...], preferred_element_type=F32).astype(BF16)
            if off < G:
                out[off - 1, pl.ds(j * DT, DT), :] = block
                d = copy(
                    out.at[off - 1, pl.ds(j * DT, DT), :],
                    inc.at[g, pl.ds(j * DT, DT), :],
                    d_ss.at[off * per + j], d_rs.at[g * per + j], (to, r),
                )
                d.start()
                row_sends.append(d)
            else:
                inc[g, pl.ds(j * DT, DT), :] = block

    for off in range(1, G):
        src = (g + off) % G
        copy(cnt.at[src], cnt.at[src], c_ss.at[off], c_rs.at[src], (src, r)).wait_recv()
    lanes = lax.broadcasted_iota(jnp.int32, (1, 128), 1)
    mine = jnp.zeros((1, 128), F32)
    n_here = []
    for q in range(G):
        n_q = jnp.sum(jnp.where(lanes == g, cnt[q], 0.0), axis=1, keepdims=True)
        n_here.append(n_q)
        mine = mine + jnp.where(lanes == q, n_q, 0.0)
    cntr[r] = mine
    rank_sends = []
    for off in range(1, R):
        to = (r + off) % R
        d = copy(cntr.at[r], cntr.at[r], k_ss.at[off], k_rs.at[r], (g, to))
        d.start()
        rank_sends.append(d)
    for off in range(1, R):
        src = (r + off) % R
        copy(cntr.at[src], cntr.at[src], k_ss.at[off], k_rs.at[src], (g, src)).wait_recv()
    total = jnp.zeros((1, 128), F32)
    early = jnp.zeros((1, 128), F32)
    for q in range(R):
        row = cntr[q]
        total = total + row
        early = early + jnp.where(r > q, row, 0.0)
    count = jnp.sum(total, axis=1, keepdims=True)
    asked = init_ref[...].astype(F32)
    wanted = asked - jnp.floor((asked + 0.5) / count) * count
    slots = lax.broadcasted_iota(jnp.int32, (1, S), 1).astype(F32)
    for q in range(G):
        base = jnp.sum(
            jnp.where(lanes < q, total, 0.0) + jnp.where(lanes == q, early, 0.0),
            axis=1, keepdims=True,
        )
        rank = jnp.where(slots < n_here[q], slots + base, -1.0)
        pick = jnp.where(wanted == rank, 1.0, 0.0).astype(BF16)
        lhst[0, :, pl.ds(q * S, S)] = pick[:H]
        lhst[1, :, pl.ds(q * S, S)] = pick[H:]

    for off in range(1, G):
        src = (g + off) % G
        for j in range(per):
            part = inc.at[src, pl.ds(j * DT, DT), :]
            copy(part, part, d_ss.at[off * per + j], d_rs.at[src * per + j], (src, r)).wait_recv()

    def half_sum(h):
        def one(q, carry):
            at = pl.ds(pl.multiple_of(q * S, S), S)
            acc[...] += jnp.dot(lhst[h, :, at], inc[q], preferred_element_type=F32)
            return carry

        acc[...] = jnp.zeros_like(acc)
        lax.fori_loop(0, G, one, 0)

    def big(t, finish, meanwhile=None):
        slot = t % 2
        half_sum(oc)
        s1s[...] = acc[...].astype(BF16)
        d1 = copy(s1s, s1r.at[slot], s1_ss.at[slot], s1_rs.at[slot], (g, partner))
        d1.start()
        half_sum(c)
        d1.wait()
        acc[...] += s1r[slot].astype(F32)
        for p in range(Z):
            s2s[p] = acc[pl.ds(p * Q, Q), :].astype(BF16)
        sends = []
        for off in range(1, Z):
            to = (z + off) % Z
            d = copy(s2s.at[to], s2r.at[slot, z], s2_ss.at[slot, off], s2_rs.at[slot, z], (g, to * 2 + c))
            d.start()
            sends.append(d)
        if meanwhile is not None:
            meanwhile()
        own = acc[pl.ds(pl.multiple_of(z * Q, Q), Q), :]
        for off in range(1, Z):
            src = (z + off) % Z
            part = s2r.at[slot, src]
            copy(part, part, s2_ss.at[slot, off], s2_rs.at[slot, src], (g, src * 2 + c)).wait_recv()
            own = own + s2r[slot, src].astype(F32)
        cent[slot, c, z] = finish(own).astype(BF16)
        for off in range(1, Z):
            to = (z + off) % Z
            d = copy(cent.at[slot, c, z], cent.at[slot, c, z], g_ss.at[slot, off], g_rs.at[slot, z], (g, to * 2 + c))
            d.start()
            sends.append(d)
        d = copy(cent.at[slot, c, z], cent.at[slot, c, z], f_ss.at[slot, z], f_rs.at[slot, z], (g, partner))
        d.start()
        sends.append(d)
        for off in range(1, Z):
            src = (z + off) % Z
            part = cent.at[slot, c, src]
            copy(part, part, g_ss.at[slot, off], g_rs.at[slot, src], (g, src * 2 + c)).wait_recv()
            d = copy(part, part, f_ss.at[slot, src], f_rs.at[slot, src], (g, partner))
            d.start()
            sends.append(d)
        for off in range(Z):
            src = (z + off) % Z
            part = cent.at[slot, oc, src]
            copy(part, part, f_ss.at[slot, src], f_rs.at[slot, src], (g, partner)).wait_recv()
        for d in sends:
            d.wait_send()

    def column_sum(t, part8):
        slot = t % 2
        cs[slot, r] = jnp.sum(part8, axis=0, keepdims=True)
        sends = []
        for off in range(1, R):
            to = (r + off) % R
            d = copy(cs.at[slot, r], cs.at[slot, r], cs_ss.at[slot, off], cs_rs.at[slot, r], (g, to))
            d.start()
            sends.append(d)
        for off in range(1, R):
            src = (r + off) % R
            part = cs.at[slot, src]
            copy(part, part, cs_ss.at[slot, off], cs_rs.at[slot, src], (g, src)).wait_recv()
        whole = cs[slot, 0]
        for q in range(1, R):
            whole = whole + cs[slot, q]
        for d in sends:
            d.wait_send()
        return whole

    tiles = N // T
    zero8 = jnp.zeros((8, K), F32)

    def down(v):
        return jnp.sum(v.reshape(T // 8, 8, K), axis=0)

    def assign_rows():
        for off in range(1, G):
            src = (g + off) % G
            part = ret.at[src]
            copy(part, part, r_ss.at[off], r_rs.at[src], (src, r)).wait_recv()

        def one(i, carry):
            at = pl.ds(pl.multiple_of(i * 256, 256), 256)
            hot = jnp.where(
                lax.broadcasted_iota(jnp.int32, (256, N), 1) == target[at, :], 1.0, 0.0
            ).astype(BF16)
            assign_ref[at, :] = jnp.dot(
                hot, ret[...].reshape(N, K), preferred_element_type=F32
            ).astype(BF16)
            return carry

        lax.fori_loop(0, tok // 256, one, 0)

    big(0, lambda v: v)
    step = 0
    back_sends = []
    for round_index in range(ROUNDS):
        last = round_index == ROUNDS - 1
        slot = round_index % 2
        part = zero8
        for q in range(G):
            n_q = n_here[q]

            def score(j, part, q=q, n_q=n_q):
                first = j * T
                v = lax.dot_general(
                    inc[q, pl.ds(pl.multiple_of(first, T), T), :],
                    cent[slot].reshape(K, E),
                    (((1,), (1,)), ((), ())), preferred_element_type=F32,
                )
                at = (lax.broadcasted_iota(jnp.int32, (T, 1), 0) + first).astype(F32)
                v = jnp.where(at < n_q, jnp.exp(v * 10.0), 0.0)
                plan[pl.ds(pl.multiple_of(q * S + first, T), T), :] = v
                return part + down(v)

            part = lax.fori_loop(0, S // T, score, part)
        for it in range(ITERS):
            col = 1.0 / column_sum(step, part)
            step += 1
            if it < ITERS - 1:

                def sweep(i, part, col=col):
                    v = plan[pl.ds(pl.multiple_of(i * T, T), T), :]
                    s = jnp.sum(v * col, axis=1, keepdims=True)
                    return part + down(v * jnp.where(s > 0.0, 1.0 / s, 0.0))

                part = lax.fori_loop(0, tiles, sweep, zero8)
            else:

                def settle(i, part, col=col):
                    at = pl.ds(pl.multiple_of(i * T, T), T)
                    v = plan[at, :] * col
                    s = jnp.sum(v, axis=1, keepdims=True)
                    v = v * jnp.where(s > 0.0, 1.0 / s, 0.0)
                    if last:
                        planb[at, :] = v.astype(BF16)
                    vt = v.T.astype(BF16)
                    lhst[0, :, at] = vt[:H]
                    lhst[1, :, at] = vt[H:]
                    return part + down(v)

                part = lax.fori_loop(0, tiles, settle, zero8)
        if not last:
            big(
                round_index + 1,
                lambda v: v * lax.rsqrt(jnp.sum(v * v, axis=1, keepdims=True) + 1e-06),
            )
        else:
            for off in range(1, G):
                to = (g + off) % G
                d = copy(
                    planb.at[pl.ds(pl.multiple_of(to * S, S), S), :], ret.at[g],
                    r_ss.at[off], r_rs.at[g], (to, r),
                )
                d.start()
                back_sends.append(d)
            ret[g] = planb[pl.ds(pl.multiple_of(g * S, S), S), :]
            weight = column_sum(step, part)
            first = c * H + z * Q
            wide = lax.broadcasted_iota(jnp.int32, (Q, K), 0) + first
            pick = wide == lax.broadcasted_iota(jnp.int32, (Q, K), 1)
            w = jnp.sum(jnp.where(pick, weight, 0.0), axis=1, keepdims=True)
            big(ROUNDS, lambda v: v / w, assign_rows)
            means_ref[...] = cent[ROUNDS % 2].reshape(K, E).astype(F32)

    for d in count_sends + row_sends + rank_sends + back_sends:
        d.wait_send()


def on_device(G, R, embeddings, labels, init_idx):
    tok, E = embeddings.shape
    K = init_idx.shape[1]
    S = 2 * tok // G
    T = min(256, S)
    N = G * S
    Z = R // 2
    Q = K // 2 // Z
    per = S // min(256, S)
    dma = pltpu.SemaphoreType.DMA
    vm = pltpu.VMEM
    assign, means = pl.pallas_call(
        functools.partial(kernel, G, R, tok, E, K, S, T),
        out_shape=(
            jax.ShapeDtypeStruct((tok, K), BF16),
            jax.ShapeDtypeStruct((K, E), F32),
        ),
        in_specs=[pl.BlockSpec(memory_space=pltpu.VMEM)] * 4,
        out_specs=[pl.BlockSpec(memory_space=pltpu.VMEM)] * 2,
        scratch_shapes=[
            vm((tok, E), BF16),
            vm((G - 1, S, E), BF16),
            vm((G, S, E), BF16),
            vm((N, K), F32),
            vm((N, K), BF16),
            vm((2, K // 2, N), BF16),
            vm((K // 2, E), F32),
            vm((G, S, K), BF16),
            vm((tok, 1), jnp.int32),
            vm((G, 1, 128), F32),
            vm((R, 1, 128), F32),
            vm((2, R, 1, K), F32),
            vm((K // 2, E), BF16),
            vm((2, K // 2, E), BF16),
            vm((Z, Q, E), BF16),
            vm((2, Z, Q, E), BF16),
            vm((2, 2, Z, Q, E), BF16),
            dma(((G + 1) * per,)), dma((G * per,)),
            dma((G,)), dma((G,)),
            dma((R,)), dma((R,)),
            dma((2, R)), dma((2, R)),
            dma((2,)), dma((2,)),
            dma((2, Z)), dma((2, Z)),
            dma((2, Z)), dma((2, Z)),
            dma((2, Z)), dma((2, Z)),
            dma((G,)), dma((G,)),
        ],
        compiler_params=pltpu.CompilerParams(
            collective_id=0, has_side_effects=True, vmem_limit_bytes=48 * 1024 * 1024,
        ),
    )(embeddings, labels.reshape(1, tok), labels, init_idx.reshape(K, 1))
    return (assign, means[None])


def solution(mesh):
    return jax.shard_map(
        functools.partial(on_device, mesh.shape["sc"], mesh.shape["rows"]),
        mesh=mesh,
        in_specs=(P(("sc", "rows"), None), P(("sc", "rows"), None), P("sc", None)),
        out_specs=(P(("sc", "rows"), None), P("sc", None, None)),
        check_vma=False,
    )
```

```python
import functools
import math

import jax
import jax.numpy as jnp
from jax import lax
from jax.experimental import pallas as pl
from jax.experimental.pallas import tpu as pltpu
from jax.sharding import PartitionSpec as P

ITERS = 3
ROUNDS = 3
MESH = pl.DeviceIdType.MESH
F32 = jnp.float32
BF16 = jnp.bfloat16


def kernel(
    G, R, tok, E, K, S, T,
    x_ref, labr_ref, init_ref,
    assign_ref, means_ref,
    xu, out, inc, plan, planb, lhst, acc, ret, target,
    cnt, cntr, cs, s1s, s1r, s2s, s2r, cent,
    d_ss, d_rs, c_ss, c_rs, k_ss, k_rs, cs_ss, cs_rs,
    s1_ss, s1_rs, s2_ss, s2_rs, g_ss, g_rs, f_ss, f_rs, r_ss, r_rs,
):
    g = lax.axis_index("sc")
    r = lax.axis_index("rows")
    Z = R // 2
    H = K // 2
    Q = H // Z
    N = G * S
    z = r // 2
    c = r % 2
    oc = 1 - c
    partner = z * 2 + oc

    def copy(src, dst, ss, rs, to):
        return pltpu.make_async_remote_copy(
            src_ref=src, dst_ref=dst, send_sem=ss, recv_sem=rs,
            device_id=to, device_id_type=MESH,
        )

    barrier = pltpu.get_barrier_semaphore()
    for off in range(1, R):
        pl.semaphore_signal(barrier, inc=1, device_id=(g, (r + off) % R), device_id_type=MESH)
    for off in range(1, G):
        pl.semaphore_signal(barrier, inc=1, device_id=((g + off) % G, r), device_id_type=MESH)

    def unit(i, carry):
        at = pl.ds(pl.multiple_of(i * 128, 128), 128)
        v = x_ref[at, :].astype(F32)
        scale = lax.rsqrt(jnp.mean(v * v, axis=1, keepdims=True) + 1e-05) * (1.0 / math.sqrt(E))
        xu[at, :] = (v * scale).astype(BF16)
        return carry

    lax.fori_loop(0, tok // 128, unit, 0)

    labr = labr_ref[...]
    sub = lax.broadcasted_iota(jnp.int32, (128, 128), 0)
    lane = lax.broadcasted_iota(jnp.int32, (128, 128), 1)
    tri = jnp.where(sub < lane, 1.0, 0.0).astype(BF16)
    mem = jnp.where(lax.broadcasted_iota(jnp.int32, (16, tok), 0) == labr, 1.0, 0.0)
    seen = jnp.zeros((16, 1), F32)
    places = []
    for b in range(tok // 128):
        part = mem[:, b * 128:(b + 1) * 128]
        before = jnp.dot(part.astype(BF16), tri, preferred_element_type=F32) + seen
        places.append(jnp.sum(before * part, axis=0, keepdims=True))
        seen = seen + jnp.sum(part, axis=1, keepdims=True)
    place_i = jnp.concatenate(places, axis=1).astype(jnp.int32)
    cnt[g] = jnp.sum(jnp.where(sub[:16] == lane[:16], seen, 0.0), axis=0, keepdims=True)

    pl.semaphore_wait(barrier, R - 1 + G - 1)

    count_sends = []
    for off in range(1, G):
        to = (g + off) % G
        d = copy(cnt.at[g], cnt.at[g], c_ss.at[off], c_rs.at[g], (to, r))
        d.start()
        count_sends.append(d)

    DT = min(256, S)
    per = S // DT
    row_sends = []
    for off in range(1, G + 1):
        to = (g + off) % G
        chosen = jnp.where(labr == to, place_i, -1)
        for j in range(per):
            slot = lax.broadcasted_iota(jnp.int32, (DT, tok), 0) + j * DT
            perm = jnp.where(slot == chosen, 1.0, 0.0).astype(BF16)
            block = jnp.dot(perm, xu[...], preferred_element_type=F32).astype(BF16)
            if off < G:
                out[off - 1, pl.ds(j * DT, DT), :] = block
                d = copy(
                    out.at[off - 1, pl.ds(j * DT, DT), :],
                    inc.at[g, pl.ds(j * DT, DT), :],
                    d_ss.at[off * per + j], d_rs.at[g * per + j], (to, r),
                )
                d.start()
                row_sends.append(d)
            else:
                inc[g, pl.ds(j * DT, DT), :] = block

    slot_of = (labr * S + place_i).astype(F32)
    for b in range(tok // 128):
        wide = jnp.broadcast_to(slot_of[:, b * 128:(b + 1) * 128], (128, 128))
        target[pl.ds(b * 128, 128), :] = wide.T[:, :1].astype(jnp.int32)

    for off in range(1, G):
        src = (g + off) % G
        copy(cnt.at[src], cnt.at[src], c_ss.at[off], c_rs.at[src], (src, r)).wait_recv()
    lanes = lax.broadcasted_iota(jnp.int32, (1, 128), 1)
    mine = jnp.zeros((1, 128), F32)
    n_here = []
    for q in range(G):
        n_q = jnp.sum(jnp.where(lanes == g, cnt[q], 0.0), axis=1, keepdims=True)
        n_here.append(n_q)
        mine = mine + jnp.where(lanes == q, n_q, 0.0)
    cntr[r] = mine
    rank_sends = []
    for off in range(1, R):
        to = (r + off) % R
        d = copy(cntr.at[r], cntr.at[r], k_ss.at[off], k_rs.at[r], (g, to))
        d.start()
        rank_sends.append(d)
    for off in range(1, R):
        src = (r + off) % R
        copy(cntr.at[src], cntr.at[src], k_ss.at[off], k_rs.at[src], (g, src)).wait_recv()
    total = jnp.zeros((1, 128), F32)
    early = jnp.zeros((1, 128), F32)
    for q in range(R):
        row = cntr[q]
        total = total + row
        early = early + jnp.where(r > q, row, 0.0)
    count = jnp.sum(total, axis=1, keepdims=True)
    asked = init_ref[...].astype(F32)
    wanted = asked - jnp.floor((asked + 0.5) / count) * count
    slots = lax.broadcasted_iota(jnp.int32, (1, S), 1).astype(F32)
    for q in range(G):
        base = jnp.sum(
            jnp.where(lanes < q, total, 0.0) + jnp.where(lanes == q, early, 0.0),
            axis=1, keepdims=True,
        )
        rank = jnp.where(slots < n_here[q], slots + base, -1.0)
        pick = jnp.where(wanted == rank, 1.0, 0.0).astype(BF16)
        lhst[0, :, pl.ds(q * S, S)] = pick[:H]
        lhst[1, :, pl.ds(q * S, S)] = pick[H:]

    for off in range(1, G):
        src = (g + off) % G
        for j in range(per):
            part = inc.at[src, pl.ds(j * DT, DT), :]
            copy(part, part, d_ss.at[off * per + j], d_rs.at[src * per + j], (src, r)).wait_recv()

    C = E // 2

    def half_sum(h, e):
        rows = inc[:, :, pl.ds(e * C, C)].reshape(N, C)
        return jnp.dot(lhst[h], rows, preferred_element_type=F32)

    def big(t, finish, meanwhile=None):
        slot = t % 2
        first = []
        sends = []
        for e in range(2):
            s1s[e] = half_sum(oc, e).astype(BF16)
            d = copy(s1s.at[e], s1r.at[slot, e], s1_ss.at[slot, e], s1_rs.at[slot, e], (g, partner))
            d.start()
            first.append(d)
        for e in range(2):
            acc[e] = half_sum(c, e)
            first[e].wait_recv()
            acc[e] += s1r[slot, e].astype(F32)
            for p in range(Z):
                s2s[e, p] = acc[e, pl.ds(p * Q, Q), :].astype(BF16)
            for off in range(1, Z):
                to = (z + off) % Z
                d = copy(
                    s2s.at[e, to], s2r.at[slot, e, z],
                    s2_ss.at[slot, e, off], s2_rs.at[slot, e, z], (g, to * 2 + c),
                )
                d.start()
                sends.append(d)
        halves = []
        for e in range(2):
            own = acc[e, pl.ds(pl.multiple_of(z * Q, Q), Q), :]
            for off in range(1, Z):
                src = (z + off) % Z
                part = s2r.at[slot, e, src]
                copy(
                    part, part, s2_ss.at[slot, e, off], s2_rs.at[slot, e, src], (g, src * 2 + c)
                ).wait_recv()
                own = own + s2r[slot, e, src].astype(F32)
            halves.append(own)
        own = jnp.concatenate(halves, axis=1)
        cent[slot, c, z] = finish(own).astype(BF16)
        for off in range(1, Z):
            to = (z + off) % Z
            d = copy(cent.at[slot, c, z], cent.at[slot, c, z], g_ss.at[slot, off], g_rs.at[slot, z], (g, to * 2 + c))
            d.start()
            sends.append(d)
        d = copy(cent.at[slot, c, z], cent.at[slot, c, z], f_ss.at[slot, z], f_rs.at[slot, z], (g, partner))
        d.start()
        sends.append(d)
        for off in range(1, Z):
            src = (z + off) % Z
            part = cent.at[slot, c, src]
            copy(part, part, g_ss.at[slot, off], g_rs.at[slot, src], (g, src * 2 + c)).wait_recv()
            d = copy(part, part, f_ss.at[slot, src], f_rs.at[slot, src], (g, partner))
            d.start()
            sends.append(d)
        if meanwhile is not None:
            meanwhile()
        for off in range(Z):
            src = (z + off) % Z
            part = cent.at[slot, oc, src]
            copy(part, part, f_ss.at[slot, src], f_rs.at[slot, src], (g, partner)).wait_recv()
        for d in first + sends:
            d.wait_send()

    def column_sum(t, part8):
        slot = t % 2
        cs[slot, r] = jnp.sum(part8, axis=0, keepdims=True)
        sends = []
        for off in range(1, R):
            to = (r + off) % R
            d = copy(cs.at[slot, r], cs.at[slot, r], cs_ss.at[slot, off], cs_rs.at[slot, r], (g, to))
            d.start()
            sends.append(d)
        for off in range(1, R):
            src = (r + off) % R
            part = cs.at[slot, src]
            copy(part, part, cs_ss.at[slot, off], cs_rs.at[slot, src], (g, src)).wait_recv()
        whole = cs[slot, 0]
        for q in range(1, R):
            whole = whole + cs[slot, q]
        for d in sends:
            d.wait_send()
        return whole

    tiles = N // T
    zero8 = jnp.zeros((8, K), F32)

    def down(v):
        return jnp.sum(v.reshape(T // 8, 8, K), axis=0)

    def assign_rows():
        for off in range(1, G):
            src = (g + off) % G
            part = ret.at[src]
            copy(part, part, r_ss.at[off], r_rs.at[src], (src, r)).wait_recv()

        def one(i, carry):
            at = pl.ds(pl.multiple_of(i * 256, 256), 256)
            hot = jnp.where(
                lax.broadcasted_iota(jnp.int32, (256, N), 1) == target[at, :], 1.0, 0.0
            ).astype(BF16)
            assign_ref[at, :] = jnp.dot(
                hot, ret[...].reshape(N, K), preferred_element_type=F32
            ).astype(BF16)
            return carry

        lax.fori_loop(0, tok // 256, one, 0)

    big(0, lambda v: v)
    step = 0
    back_sends = []
    for round_index in range(ROUNDS):
        last = round_index == ROUNDS - 1
        slot = round_index % 2
        part = zero8
        for q in range(G):
            n_q = n_here[q]

            def score(j, part, q=q, n_q=n_q):
                first = j * T
                v = lax.dot_general(
                    inc[q, pl.ds(pl.multiple_of(first, T), T), :],
                    cent[slot].reshape(K, E),
                    (((1,), (1,)), ((), ())), preferred_element_type=F32,
                )
                at = (lax.broadcasted_iota(jnp.int32, (T, 1), 0) + first).astype(F32)
                v = jnp.where(at < n_q, jnp.exp(v * 10.0), 0.0)
                plan[pl.ds(pl.multiple_of(q * S + first, T), T), :] = v
                return part + down(v)

            part = lax.fori_loop(0, S // T, score, part)
        for it in range(ITERS):
            col = 1.0 / column_sum(step, part)
            step += 1
            if it < ITERS - 1:

                def sweep(i, part, col=col):
                    v = plan[pl.ds(pl.multiple_of(i * T, T), T), :]
                    s = jnp.sum(v * col, axis=1, keepdims=True)
                    return part + down(v * jnp.where(s > 0.0, 1.0 / s, 0.0))

                part = lax.fori_loop(0, tiles, sweep, zero8)
            else:

                def settle(i, part, col=col):
                    at = pl.ds(pl.multiple_of(i * T, T), T)
                    v = plan[at, :] * col
                    s = jnp.sum(v, axis=1, keepdims=True)
                    v = v * jnp.where(s > 0.0, 1.0 / s, 0.0)
                    if last:
                        planb[at, :] = v.astype(BF16)
                    vt = v.T.astype(BF16)
                    lhst[0, :, at] = vt[:H]
                    lhst[1, :, at] = vt[H:]
                    return part + down(v)

                part = lax.fori_loop(0, tiles, settle, zero8)
        if not last:
            big(
                round_index + 1,
                lambda v: v * lax.rsqrt(jnp.sum(v * v, axis=1, keepdims=True) + 1e-06),
            )
        else:
            for off in range(1, G):
                to = (g + off) % G
                d = copy(
                    planb.at[pl.ds(pl.multiple_of(to * S, S), S), :], ret.at[g],
                    r_ss.at[off], r_rs.at[g], (to, r),
                )
                d.start()
                back_sends.append(d)
            ret[g] = planb[pl.ds(pl.multiple_of(g * S, S), S), :]
            weight = column_sum(step, part)
            first = c * H + z * Q
            wide = lax.broadcasted_iota(jnp.int32, (Q, K), 0) + first
            pick = wide == lax.broadcasted_iota(jnp.int32, (Q, K), 1)
            w = jnp.sum(jnp.where(pick, weight, 0.0), axis=1, keepdims=True)
            big(ROUNDS, lambda v: v / w, assign_rows)
            means_ref[...] = cent[ROUNDS % 2].reshape(K, E).astype(F32)

    for d in count_sends + row_sends + rank_sends + back_sends:
        d.wait_send()


def on_device(G, R, embeddings, labels, init_idx):
    tok, E = embeddings.shape
    K = init_idx.shape[1]
    S = 2 * tok // G
    T = min(256, S)
    N = G * S
    Z = R // 2
    Q = K // 2 // Z
    per = S // min(256, S)
    dma = pltpu.SemaphoreType.DMA
    vm = pltpu.VMEM
    assign, means = pl.pallas_call(
        functools.partial(kernel, G, R, tok, E, K, S, T),
        out_shape=(
            jax.ShapeDtypeStruct((tok, K), BF16),
            jax.ShapeDtypeStruct((K, E), F32),
        ),
        in_specs=[pl.BlockSpec(memory_space=pltpu.VMEM)] * 3,
        out_specs=[pl.BlockSpec(memory_space=pltpu.VMEM)] * 2,
        scratch_shapes=[
            vm((tok, E), BF16),
            vm((G - 1, S, E), BF16),
            vm((G, S, E), BF16),
            vm((N, K), F32),
            vm((N, K), BF16),
            vm((2, K // 2, N), BF16),
            vm((2, K // 2, E // 2), F32),
            vm((G, S, K), BF16),
            vm((tok, 1), jnp.int32),
            vm((G, 1, 128), F32),
            vm((R, 1, 128), F32),
            vm((2, R, 1, K), F32),
            vm((2, K // 2, E // 2), BF16),
            vm((2, 2, K // 2, E // 2), BF16),
            vm((2, Z, Q, E // 2), BF16),
            vm((2, 2, Z, Q, E // 2), BF16),
            vm((2, 2, Z, Q, E), BF16),
            dma(((G + 1) * per,)), dma((G * per,)),
            dma((G,)), dma((G,)),
            dma((R,)), dma((R,)),
            dma((2, R)), dma((2, R)),
            dma((2, 2)), dma((2, 2)),
            dma((2, 2, Z)), dma((2, 2, Z)),
            dma((2, Z)), dma((2, Z)),
            dma((2, Z)), dma((2, Z)),
            dma((G,)), dma((G,)),
        ],
        compiler_params=pltpu.CompilerParams(
            collective_id=0, has_side_effects=True, vmem_limit_bytes=48 * 1024 * 1024,
        ),
    )(embeddings, labels.reshape(1, tok), init_idx.reshape(K, 1))
    return (assign, means[None])


def solution(mesh):
    return jax.shard_map(
        functools.partial(on_device, mesh.shape["sc"], mesh.shape["rows"]),
        mesh=mesh,
        in_specs=(P(("sc", "rows"), None), P(("sc", "rows"), None), P("sc", None)),
        out_specs=(P(("sc", "rows"), None), P("sc", None, None)),
        check_vma=False,
    )
```

```python
import functools
import math

import jax
import jax.numpy as jnp
from jax import lax
from jax.experimental import pallas as pl
from jax.experimental.pallas import tpu as pltpu
from jax.sharding import PartitionSpec as P

ITERS = 3
ROUNDS = 3
MESH = pl.DeviceIdType.MESH
F32 = jnp.float32
BF16 = jnp.bfloat16


def kernel(
    G, R, tok, E, K, S, T,
    x_ref, labr_ref, init_ref,
    assign_ref, means_ref,
    xu, out, inc, plan, planb, lhst, acc, ret, target,
    cnt, cntr, cs, s1s, s1r, s2s, s2r, cent,
    d_ss, d_rs, c_ss, c_rs, k_ss, k_rs, cs_ss, cs_rs,
    s1_ss, s1_rs, s2_ss, s2_rs, g_ss, g_rs, f_ss, f_rs, r_ss, r_rs,
):
    g = lax.axis_index("sc")
    r = lax.axis_index("rows")
    Z = R // 2
    H = K // 2
    Q = H // Z
    N = G * S
    z = r // 2
    c = r % 2
    oc = 1 - c
    partner = z * 2 + oc

    def copy(src, dst, ss, rs, to):
        return pltpu.make_async_remote_copy(
            src_ref=src, dst_ref=dst, send_sem=ss, recv_sem=rs,
            device_id=to, device_id_type=MESH,
        )

    barrier = pltpu.get_barrier_semaphore()
    for off in range(1, R):
        pl.semaphore_signal(barrier, inc=1, device_id=(g, (r + off) % R), device_id_type=MESH)
    for off in range(1, G):
        pl.semaphore_signal(barrier, inc=1, device_id=((g + off) % G, r), device_id_type=MESH)

    def unit(i, carry):
        at = pl.ds(pl.multiple_of(i * 128, 128), 128)
        v = x_ref[at, :].astype(F32)
        scale = lax.rsqrt(jnp.mean(v * v, axis=1, keepdims=True) + 1e-05) * (1.0 / math.sqrt(E))
        xu[at, :] = (v * scale).astype(BF16)
        return carry

    lax.fori_loop(0, tok // 128, unit, 0)

    labr = labr_ref[...]
    sub = lax.broadcasted_iota(jnp.int32, (128, 128), 0)
    lane = lax.broadcasted_iota(jnp.int32, (128, 128), 1)
    tri = jnp.where(sub < lane, 1.0, 0.0).astype(BF16)
    mem = jnp.where(lax.broadcasted_iota(jnp.int32, (16, tok), 0) == labr, 1.0, 0.0)
    seen = jnp.zeros((16, 1), F32)
    places = []
    for b in range(tok // 128):
        part = mem[:, b * 128:(b + 1) * 128]
        before = jnp.dot(part.astype(BF16), tri, preferred_element_type=F32) + seen
        places.append(jnp.sum(before * part, axis=0, keepdims=True))
        seen = seen + jnp.sum(part, axis=1, keepdims=True)
    place_i = jnp.concatenate(places, axis=1).astype(jnp.int32)
    cnt[g] = jnp.sum(jnp.where(sub[:16] == lane[:16], seen, 0.0), axis=0, keepdims=True)

    pl.semaphore_wait(barrier, R - 1 + G - 1)

    count_sends = []
    for off in range(1, G):
        to = (g + off) % G
        d = copy(cnt.at[g], cnt.at[g], c_ss.at[off], c_rs.at[g], (to, r))
        d.start()
        count_sends.append(d)

    DT = min(128, S)
    per = S // DT
    row_sends = []
    chosen = [jnp.where(labr == (g + off) % G, place_i, -1) for off in range(1, G + 1)]
    for j, off in [(j, off) for j in range(per) for off in range(1, G)] + [(j, G) for j in range(per)]:
        at = pl.ds(j * DT, DT)
        slot = lax.broadcasted_iota(jnp.int32, (DT, tok), 0) + j * DT
        perm = jnp.where(slot == chosen[off - 1], 1.0, 0.0).astype(BF16)
        block = jnp.dot(perm, xu[...], preferred_element_type=F32).astype(BF16)
        if off < G:
            out[off - 1, at, :] = block
            d = copy(
                out.at[off - 1, at, :], inc.at[g, at, :],
                d_ss.at[off * per + j], d_rs.at[g * per + j], ((g + off) % G, r),
            )
            d.start()
            row_sends.append(d)
        else:
            inc[g, at, :] = block

    slot_of = (labr * S + place_i).astype(F32)
    for b in range(tok // 128):
        wide = jnp.broadcast_to(slot_of[:, b * 128:(b + 1) * 128], (128, 128))
        target[pl.ds(b * 128, 128), :] = wide.T[:, :1].astype(jnp.int32)

    for off in range(1, G):
        src = (g + off) % G
        copy(cnt.at[src], cnt.at[src], c_ss.at[off], c_rs.at[src], (src, r)).wait_recv()
    lanes = lax.broadcasted_iota(jnp.int32, (1, 128), 1)
    mine = jnp.zeros((1, 128), F32)
    n_here = []
    for q in range(G):
        n_q = jnp.sum(jnp.where(lanes == g, cnt[q], 0.0), axis=1, keepdims=True)
        n_here.append(n_q)
        mine = mine + jnp.where(lanes == q, n_q, 0.0)
    cntr[r] = mine
    rank_sends = []
    for off in range(1, R):
        to = (r + off) % R
        d = copy(cntr.at[r], cntr.at[r], k_ss.at[off], k_rs.at[r], (g, to))
        d.start()
        rank_sends.append(d)
    for off in range(1, R):
        src = (r + off) % R
        copy(cntr.at[src], cntr.at[src], k_ss.at[off], k_rs.at[src], (g, src)).wait_recv()
    total = jnp.zeros((1, 128), F32)
    early = jnp.zeros((1, 128), F32)
    for q in range(R):
        row = cntr[q]
        total = total + row
        early = early + jnp.where(r > q, row, 0.0)
    count = jnp.sum(total, axis=1, keepdims=True)
    asked = init_ref[...].astype(F32)
    wanted = asked - jnp.floor((asked + 0.5) / count) * count
    slots = lax.broadcasted_iota(jnp.int32, (1, S), 1).astype(F32)
    for q in range(G):
        base = jnp.sum(
            jnp.where(lanes < q, total, 0.0) + jnp.where(lanes == q, early, 0.0),
            axis=1, keepdims=True,
        )
        rank = jnp.where(slots < n_here[q], slots + base, -1.0)
        pick = jnp.where(wanted == rank, 1.0, 0.0).astype(BF16)
        lhst[0, :, pl.ds(q * S, S)] = pick[:H]
        lhst[1, :, pl.ds(q * S, S)] = pick[H:]

    for off in range(1, G):
        src = (g + off) % G
        for j in range(per):
            part = inc.at[src, pl.ds(j * DT, DT), :]
            copy(part, part, d_ss.at[off * per + j], d_rs.at[src * per + j], (src, r)).wait_recv()

    C = E // 2

    def half_sum(h, e):
        rows = inc[:, :, pl.ds(e * C, C)].reshape(N, C)
        return jnp.dot(lhst[h], rows, preferred_element_type=F32)

    def big(t, finish, meanwhile=None):
        slot = t % 2
        first = []
        sends = []
        for e in range(2):
            s1s[e] = half_sum(oc, e).astype(BF16)
            d = copy(s1s.at[e], s1r.at[slot, e], s1_ss.at[slot, e], s1_rs.at[slot, e], (g, partner))
            d.start()
            first.append(d)
        for e in range(2):
            acc[e] = half_sum(c, e)
            first[e].wait_recv()
            acc[e] += s1r[slot, e].astype(F32)
            for p in range(Z):
                s2s[e, p] = acc[e, pl.ds(p * Q, Q), :].astype(BF16)
            for off in range(1, Z):
                to = (z + off) % Z
                d = copy(
                    s2s.at[e, to], s2r.at[slot, e, z],
                    s2_ss.at[slot, e, off], s2_rs.at[slot, e, z], (g, to * 2 + c),
                )
                d.start()
                sends.append(d)
        halves = []
        for e in range(2):
            own = acc[e, pl.ds(pl.multiple_of(z * Q, Q), Q), :]
            for off in range(1, Z):
                src = (z + off) % Z
                part = s2r.at[slot, e, src]
                copy(
                    part, part, s2_ss.at[slot, e, off], s2_rs.at[slot, e, src], (g, src * 2 + c)
                ).wait_recv()
                own = own + s2r[slot, e, src].astype(F32)
            halves.append(own)
        own = jnp.concatenate(halves, axis=1)
        cent[slot, c, z] = finish(own).astype(BF16)
        for off in range(1, Z):
            to = (z + off) % Z
            d = copy(cent.at[slot, c, z], cent.at[slot, c, z], g_ss.at[slot, off], g_rs.at[slot, z], (g, to * 2 + c))
            d.start()
            sends.append(d)
        d = copy(cent.at[slot, c, z], cent.at[slot, c, z], f_ss.at[slot, z], f_rs.at[slot, z], (g, partner))
        d.start()
        sends.append(d)
        if meanwhile is not None:
            meanwhile()
        for off in range(1, Z):
            src = (z + off) % Z
            part = cent.at[slot, c, src]
            copy(part, part, g_ss.at[slot, off], g_rs.at[slot, src], (g, src * 2 + c)).wait_recv()
            d = copy(part, part, f_ss.at[slot, src], f_rs.at[slot, src], (g, partner))
            d.start()
            sends.append(d)
        for off in range(Z):
            src = (z + off) % Z
            part = cent.at[slot, oc, src]
            copy(part, part, f_ss.at[slot, src], f_rs.at[slot, src], (g, partner)).wait_recv()
        for d in first + sends:
            d.wait_send()

    def column_start(t, part8):
        slot = t % 2
        cs[slot, r] = jnp.sum(part8, axis=0, keepdims=True)
        sends = []
        for off in range(1, R):
            to = (r + off) % R
            d = copy(cs.at[slot, r], cs.at[slot, r], cs_ss.at[slot, off], cs_rs.at[slot, r], (g, to))
            d.start()
            sends.append(d)
        return sends

    def column_sum(t, sends):
        slot = t % 2
        for off in range(1, R):
            src = (r + off) % R
            part = cs.at[slot, src]
            copy(part, part, cs_ss.at[slot, off], cs_rs.at[slot, src], (g, src)).wait_recv()
        whole = cs[slot, 0]
        for q in range(1, R):
            whole = whole + cs[slot, q]
        for d in sends:
            d.wait_send()
        return whole

    tiles = N // T
    zero8 = jnp.zeros((8, K), F32)

    def down(v):
        return jnp.sum(v.reshape(T // 8, 8, K), axis=0)

    def assign_rows():
        for off in range(1, G):
            src = (g + off) % G
            part = ret.at[src]
            copy(part, part, r_ss.at[off], r_rs.at[src], (src, r)).wait_recv()

        def one(i, carry):
            at = pl.ds(pl.multiple_of(i * 256, 256), 256)
            hot = jnp.where(
                lax.broadcasted_iota(jnp.int32, (256, N), 1) == target[at, :], 1.0, 0.0
            ).astype(BF16)
            assign_ref[at, :] = jnp.dot(
                hot, ret[...].reshape(N, K), preferred_element_type=F32
            ).astype(BF16)
            return carry

        lax.fori_loop(0, tok // 256, one, 0)

    big(0, lambda v: v)
    step = 0
    back_sends = []
    for round_index in range(ROUNDS):
        last = round_index == ROUNDS - 1
        slot = round_index % 2
        part = zero8
        for q in range(G):
            n_q = n_here[q]

            def score(j, part, q=q, n_q=n_q):
                first = j * T
                v = lax.dot_general(
                    inc[q, pl.ds(pl.multiple_of(first, T), T), :],
                    cent[slot].reshape(K, E),
                    (((1,), (1,)), ((), ())), preferred_element_type=F32,
                )
                at = (lax.broadcasted_iota(jnp.int32, (T, 1), 0) + first).astype(F32)
                v = jnp.where(at < n_q, jnp.exp(v * 10.0), 0.0)
                plan[pl.ds(pl.multiple_of(q * S + first, T), T), :] = v
                return part + down(v)

            part = lax.fori_loop(0, S // T, score, part)
        for it in range(ITERS):
            col = 1.0 / column_sum(step, column_start(step, part))
            step += 1
            if it < ITERS - 1:

                def sweep(i, part, col=col):
                    v = plan[pl.ds(pl.multiple_of(i * T, T), T), :]
                    s = jnp.sum(v * col, axis=1, keepdims=True)
                    return part + down(v * jnp.where(s > 0.0, 1.0 / s, 0.0))

                part = lax.fori_loop(0, tiles, sweep, zero8)
            else:

                def settle(i, part, col=col):
                    at = pl.ds(pl.multiple_of(i * T, T), T)
                    v = plan[at, :] * col
                    s = jnp.sum(v, axis=1, keepdims=True)
                    v = v * jnp.where(s > 0.0, 1.0 / s, 0.0)
                    if last:
                        planb[at, :] = v.astype(BF16)
                    vt = v.T.astype(BF16)
                    lhst[0, :, at] = vt[:H]
                    lhst[1, :, at] = vt[H:]
                    return part + down(v)

                part = lax.fori_loop(0, tiles, settle, zero8)
        if not last:
            big(
                round_index + 1,
                lambda v: v * lax.rsqrt(jnp.sum(v * v, axis=1, keepdims=True) + 1e-06),
            )
        else:
            for off in range(1, G):
                to = (g + off) % G
                d = copy(
                    planb.at[pl.ds(pl.multiple_of(to * S, S), S), :], ret.at[g],
                    r_ss.at[off], r_rs.at[g], (to, r),
                )
                d.start()
                back_sends.append(d)
            ret[g] = planb[pl.ds(pl.multiple_of(g * S, S), S), :]
            weight_sends = column_start(step, part)

            def mean_of(v):
                weight = column_sum(step, weight_sends)
                wide = lax.broadcasted_iota(jnp.int32, (Q, K), 0) + (c * H + z * Q)
                pick = wide == lax.broadcasted_iota(jnp.int32, (Q, K), 1)
                return v / jnp.sum(jnp.where(pick, weight, 0.0), axis=1, keepdims=True)

            big(ROUNDS, mean_of, assign_rows)
            means_ref[...] = cent[ROUNDS % 2].reshape(K, E).astype(F32)

    for d in count_sends + row_sends + rank_sends + back_sends:
        d.wait_send()


def on_device(G, R, embeddings, labels, init_idx):
    tok, E = embeddings.shape
    K = init_idx.shape[1]
    S = 2 * tok // G
    T = min(256, S)
    N = G * S
    Z = R // 2
    Q = K // 2 // Z
    per = S // min(128, S)
    dma = pltpu.SemaphoreType.DMA
    vm = pltpu.VMEM
    assign, means = pl.pallas_call(
        functools.partial(kernel, G, R, tok, E, K, S, T),
        out_shape=(
            jax.ShapeDtypeStruct((tok, K), BF16),
            jax.ShapeDtypeStruct((K, E), F32),
        ),
        in_specs=[pl.BlockSpec(memory_space=pltpu.VMEM)] * 3,
        out_specs=[pl.BlockSpec(memory_space=pltpu.VMEM)] * 2,
        scratch_shapes=[
            vm((tok, E), BF16),
            vm((G - 1, S, E), BF16),
            vm((G, S, E), BF16),
            vm((N, K), F32),
            vm((N, K), BF16),
            vm((2, K // 2, N), BF16),
            vm((2, K // 2, E // 2), F32),
            vm((G, S, K), BF16),
            vm((tok, 1), jnp.int32),
            vm((G, 1, 128), F32),
            vm((R, 1, 128), F32),
            vm((2, R, 1, K), F32),
            vm((2, K // 2, E // 2), BF16),
            vm((2, 2, K // 2, E // 2), BF16),
            vm((2, Z, Q, E // 2), BF16),
            vm((2, 2, Z, Q, E // 2), BF16),
            vm((2, 2, Z, Q, E), BF16),
            dma(((G + 1) * per,)), dma((G * per,)),
            dma((G,)), dma((G,)),
            dma((R,)), dma((R,)),
            dma((2, R)), dma((2, R)),
            dma((2, 2)), dma((2, 2)),
            dma((2, 2, Z)), dma((2, 2, Z)),
            dma((2, Z)), dma((2, Z)),
            dma((2, Z)), dma((2, Z)),
            dma((G,)), dma((G,)),
        ],
        compiler_params=pltpu.CompilerParams(
            collective_id=0, has_side_effects=True, vmem_limit_bytes=48 * 1024 * 1024,
        ),
    )(embeddings, labels.reshape(1, tok), init_idx.reshape(K, 1))
    return (assign, means[None])


def solution(mesh):
    return jax.shard_map(
        functools.partial(on_device, mesh.shape["sc"], mesh.shape["rows"]),
        mesh=mesh,
        in_specs=(P(("sc", "rows"), None), P(("sc", "rows"), None), P("sc", None)),
        out_specs=(P(("sc", "rows"), None), P("sc", None, None)),
        check_vma=False,
    )
```

```python
import functools
import math

import jax
import jax.numpy as jnp
from jax import lax
from jax.experimental import pallas as pl
from jax.experimental.pallas import tpu as pltpu
from jax.sharding import PartitionSpec as P

ITERS = 3
ROUNDS = 3
MESH = pl.DeviceIdType.MESH
F32 = jnp.float32
BF16 = jnp.bfloat16


def kernel(
    G, R, tok, E, K, S, T,
    x_ref, labr_ref, init_ref,
    assign_ref, means_ref,
    xu, out, inc, plan, planb, lhst, acc, ret, target,
    cnt, cntr, cs, s1s, s1r, s2s, s2r, cent,
    d_ss, d_rs, c_ss, c_rs, k_ss, k_rs, cs_ss, cs_rs,
    s1_ss, s1_rs, s2_ss, s2_rs, g_ss, g_rs, f_ss, f_rs, r_ss, r_rs,
):
    g = lax.axis_index("sc")
    r = lax.axis_index("rows")
    Z = R // 2
    H = K // 2
    Q = H // Z
    N = G * S
    z = r // 2
    c = r % 2
    oc = 1 - c
    partner = z * 2 + oc

    def copy(src, dst, ss, rs, to):
        return pltpu.make_async_remote_copy(
            src_ref=src, dst_ref=dst, send_sem=ss, recv_sem=rs,
            device_id=to, device_id_type=MESH,
        )

    barrier = pltpu.get_barrier_semaphore()
    for off in range(1, R):
        pl.semaphore_signal(barrier, inc=1, device_id=(g, (r + off) % R), device_id_type=MESH)
    for off in range(1, G):
        pl.semaphore_signal(barrier, inc=1, device_id=((g + off) % G, r), device_id_type=MESH)

    def unit(i, carry):
        at = pl.ds(pl.multiple_of(i * 128, 128), 128)
        v = x_ref[at, :].astype(F32)
        scale = lax.rsqrt(jnp.mean(v * v, axis=1, keepdims=True) + 1e-05) * (1.0 / math.sqrt(E))
        xu[at, :] = (v * scale).astype(BF16)
        return carry

    lax.fori_loop(0, tok // 128, unit, 0)

    labr = labr_ref[...]
    sub = lax.broadcasted_iota(jnp.int32, (128, 128), 0)
    lane = lax.broadcasted_iota(jnp.int32, (128, 128), 1)
    tri = jnp.where(sub < lane, 1.0, 0.0).astype(BF16)
    mem = jnp.where(lax.broadcasted_iota(jnp.int32, (16, tok), 0) == labr, 1.0, 0.0)
    seen = jnp.zeros((16, 1), F32)
    places = []
    for b in range(tok // 128):
        part = mem[:, b * 128:(b + 1) * 128]
        before = jnp.dot(part.astype(BF16), tri, preferred_element_type=F32) + seen
        places.append(jnp.sum(before * part, axis=0, keepdims=True))
        seen = seen + jnp.sum(part, axis=1, keepdims=True)
    place_i = jnp.concatenate(places, axis=1).astype(jnp.int32)
    cnt[g] = jnp.sum(jnp.where(sub[:16] == lane[:16], seen, 0.0), axis=0, keepdims=True)

    pl.semaphore_wait(barrier, R - 1 + G - 1)

    count_sends = []
    for off in range(1, G):
        to = (g + off) % G
        d = copy(cnt.at[g], cnt.at[g], c_ss.at[off], c_rs.at[g], (to, r))
        d.start()
        count_sends.append(d)

    DT = min(128, S)
    per = S // DT
    row_sends = []
    chosen = [jnp.where(labr == (g + off) % G, place_i, -1) for off in range(1, G + 1)]
    for j, off in [(j, off) for j in range(per) for off in range(1, G)] + [(j, G) for j in range(per)]:
        at = pl.ds(j * DT, DT)
        slot = lax.broadcasted_iota(jnp.int32, (DT, tok), 0) + j * DT
        perm = jnp.where(slot == chosen[off - 1], 1.0, 0.0).astype(BF16)
        block = jnp.dot(perm, xu[...], preferred_element_type=F32).astype(BF16)
        if off < G:
            out[off - 1, at, :] = block
            d = copy(
                out.at[off - 1, at, :], inc.at[g, at, :],
                d_ss.at[off * per + j], d_rs.at[g * per + j], ((g + off) % G, r),
            )
            d.start()
            row_sends.append(d)
        else:
            inc[g, at, :] = block

    slot_of = (labr * S + place_i).astype(F32)
    for b in range(tok // 128):
        wide = jnp.broadcast_to(slot_of[:, b * 128:(b + 1) * 128], (128, 128))
        target[pl.ds(b * 128, 128), :] = wide.T[:, :1].astype(jnp.int32)

    for off in range(1, G):
        src = (g + off) % G
        copy(cnt.at[src], cnt.at[src], c_ss.at[off], c_rs.at[src], (src, r)).wait_recv()
    lanes = lax.broadcasted_iota(jnp.int32, (1, 128), 1)
    mine = jnp.zeros((1, 128), F32)
    n_here = []
    for q in range(G):
        n_q = jnp.sum(jnp.where(lanes == g, cnt[q], 0.0), axis=1, keepdims=True)
        n_here.append(n_q)
        mine = mine + jnp.where(lanes == q, n_q, 0.0)
    cntr[r] = mine
    rank_sends = []
    for off in range(1, R):
        to = (r + off) % R
        d = copy(cntr.at[r], cntr.at[r], k_ss.at[off], k_rs.at[r], (g, to))
        d.start()
        rank_sends.append(d)
    for off in range(1, R):
        src = (r + off) % R
        copy(cntr.at[src], cntr.at[src], k_ss.at[off], k_rs.at[src], (g, src)).wait_recv()
    total = jnp.zeros((1, 128), F32)
    early = jnp.zeros((1, 128), F32)
    for q in range(R):
        row = cntr[q]
        total = total + row
        early = early + jnp.where(r > q, row, 0.0)
    count = jnp.sum(total, axis=1, keepdims=True)
    asked = init_ref[...].astype(F32)
    wanted = asked - jnp.floor((asked + 0.5) / count) * count
    slots = lax.broadcasted_iota(jnp.int32, (1, S), 1).astype(F32)
    for q in range(G):
        base = jnp.sum(
            jnp.where(lanes < q, total, 0.0) + jnp.where(lanes == q, early, 0.0),
            axis=1, keepdims=True,
        )
        rank = jnp.where(slots < n_here[q], slots + base, -1.0)
        pick = jnp.where(wanted == rank, 1.0, 0.0).astype(BF16)
        lhst[0, :, pl.ds(q * S, S)] = pick[:H]
        lhst[1, :, pl.ds(q * S, S)] = pick[H:]

    for off in range(1, G):
        src = (g + off) % G
        for j in range(per):
            part = inc.at[src, pl.ds(j * DT, DT), :]
            copy(part, part, d_ss.at[off * per + j], d_rs.at[src * per + j], (src, r)).wait_recv()

    C = E // 2

    def half_sum(h, e):
        rows = inc[:, :, pl.ds(e * C, C)].reshape(N, C)
        return jnp.dot(lhst[h], rows, preferred_element_type=F32)

    def big(t, finish, meanwhile=None):
        slot = t % 2
        first = []
        sends = []
        for e in range(2):
            s1s[e] = half_sum(oc, e).astype(BF16)
            d = copy(s1s.at[e], s1r.at[slot, e], s1_ss.at[slot, e], s1_rs.at[slot, e], (g, partner))
            d.start()
            first.append(d)
        for e in range(2):
            acc[e] = half_sum(c, e)
            first[e].wait_recv()
            acc[e] += s1r[slot, e].astype(F32)
            for p in range(Z):
                s2s[e, p] = acc[e, pl.ds(p * Q, Q), :].astype(BF16)
            for off in range(1, Z):
                to = (z + off) % Z
                d = copy(
                    s2s.at[e, to], s2r.at[slot, e, z],
                    s2_ss.at[slot, e, off], s2_rs.at[slot, e, z], (g, to * 2 + c),
                )
                d.start()
                sends.append(d)
        halves = []
        for e in range(2):
            own = acc[e, pl.ds(pl.multiple_of(z * Q, Q), Q), :]
            for off in range(1, Z):
                src = (z + off) % Z
                part = s2r.at[slot, e, src]
                copy(
                    part, part, s2_ss.at[slot, e, off], s2_rs.at[slot, e, src], (g, src * 2 + c)
                ).wait_recv()
                own = own + s2r[slot, e, src].astype(F32)
            halves.append(own)
        own = jnp.concatenate(halves, axis=1)
        cent[slot, c, z] = finish(own).astype(BF16)
        for off in range(1, Z):
            to = (z + off) % Z
            d = copy(cent.at[slot, c, z], cent.at[slot, c, z], g_ss.at[slot, off], g_rs.at[slot, z], (g, to * 2 + c))
            d.start()
            sends.append(d)
        d = copy(cent.at[slot, c, z], cent.at[slot, c, z], f_ss.at[slot, z], f_rs.at[slot, z], (g, partner))
        d.start()
        sends.append(d)
        if meanwhile is not None:
            meanwhile()
        for off in range(1, Z):
            src = (z + off) % Z
            part = cent.at[slot, c, src]
            copy(part, part, g_ss.at[slot, off], g_rs.at[slot, src], (g, src * 2 + c)).wait_recv()
            d = copy(part, part, f_ss.at[slot, src], f_rs.at[slot, src], (g, partner))
            d.start()
            sends.append(d)
        for off in range(Z):
            src = (z + off) % Z
            part = cent.at[slot, oc, src]
            copy(part, part, f_ss.at[slot, src], f_rs.at[slot, src], (g, partner)).wait_recv()
        for d in first + sends:
            d.wait_send()

    def column_start(t, part8):
        slot = t % 2
        cs[slot, r] = jnp.sum(part8, axis=0, keepdims=True)
        sends = []
        for off in sorted(range(1, R), key=lambda o: -min(o, R - o)):
            to = (r + off) % R
            d = copy(cs.at[slot, r], cs.at[slot, r], cs_ss.at[slot, off], cs_rs.at[slot, r], (g, to))
            d.start()
            sends.append(d)
        return sends

    def column_sum(t, sends):
        slot = t % 2
        for off in range(1, R):
            src = (r + off) % R
            part = cs.at[slot, src]
            copy(part, part, cs_ss.at[slot, off], cs_rs.at[slot, src], (g, src)).wait_recv()
        whole = cs[slot, 0]
        for q in range(1, R):
            whole = whole + cs[slot, q]
        for d in sends:
            d.wait_send()
        return whole

    tiles = N // T
    zero8 = jnp.zeros((8, K), F32)

    def down(v):
        return jnp.sum(v.reshape(T // 8, 8, K), axis=0)

    def assign_rows():
        for off in range(1, G):
            src = (g + off) % G
            part = ret.at[src]
            copy(part, part, r_ss.at[off], r_rs.at[src], (src, r)).wait_recv()

        def one(i, carry):
            at = pl.ds(pl.multiple_of(i * 256, 256), 256)
            hot = jnp.where(
                lax.broadcasted_iota(jnp.int32, (256, N), 1) == target[at, :], 1.0, 0.0
            ).astype(BF16)
            assign_ref[at, :] = jnp.dot(
                hot, ret[...].reshape(N, K), preferred_element_type=F32
            ).astype(BF16)
            return carry

        lax.fori_loop(0, tok // 256, one, 0)

    big(0, lambda v: v)
    step = 0
    back_sends = []
    for round_index in range(ROUNDS):
        last = round_index == ROUNDS - 1
        slot = round_index % 2
        part = zero8
        for q in range(G):
            n_q = n_here[q]

            def score(j, part, q=q, n_q=n_q):
                first = j * T
                v = lax.dot_general(
                    inc[q, pl.ds(pl.multiple_of(first, T), T), :],
                    cent[slot].reshape(K, E),
                    (((1,), (1,)), ((), ())), preferred_element_type=F32,
                )
                at = (lax.broadcasted_iota(jnp.int32, (T, 1), 0) + first).astype(F32)
                v = jnp.where(at < n_q, jnp.exp(v * 10.0), 0.0)
                plan[pl.ds(pl.multiple_of(q * S + first, T), T), :] = v
                return part + down(v)

            part = lax.fori_loop(0, S // T, score, part)
        for it in range(ITERS):
            col = 1.0 / column_sum(step, column_start(step, part))
            step += 1
            if it < ITERS - 1:

                def sweep(i, part, col=col):
                    v = plan[pl.ds(pl.multiple_of(i * T, T), T), :]
                    s = jnp.sum(v * col, axis=1, keepdims=True)
                    return part + down(v * jnp.where(s > 0.0, 1.0 / s, 0.0))

                part = lax.fori_loop(0, tiles, sweep, zero8)
            else:

                def settle(i, part, col=col):
                    at = pl.ds(pl.multiple_of(i * T, T), T)
                    v = plan[at, :] * col
                    s = jnp.sum(v, axis=1, keepdims=True)
                    v = v * jnp.where(s > 0.0, 1.0 / s, 0.0)
                    if last:
                        planb[at, :] = v.astype(BF16)
                    vt = v.T.astype(BF16)
                    lhst[0, :, at] = vt[:H]
                    lhst[1, :, at] = vt[H:]
                    return part + down(v)

                part = lax.fori_loop(0, tiles, settle, zero8)
        if not last:
            big(
                round_index + 1,
                lambda v: v * lax.rsqrt(jnp.sum(v * v, axis=1, keepdims=True) + 1e-06),
            )
        else:
            for off in range(1, G):
                to = (g + off) % G
                d = copy(
                    planb.at[pl.ds(pl.multiple_of(to * S, S), S), :], ret.at[g],
                    r_ss.at[off], r_rs.at[g], (to, r),
                )
                d.start()
                back_sends.append(d)
            ret[g] = planb[pl.ds(pl.multiple_of(g * S, S), S), :]
            weight_sends = column_start(step, part)

            def mean_of(v):
                weight = column_sum(step, weight_sends)
                wide = lax.broadcasted_iota(jnp.int32, (Q, K), 0) + (c * H + z * Q)
                pick = wide == lax.broadcasted_iota(jnp.int32, (Q, K), 1)
                return v / jnp.sum(jnp.where(pick, weight, 0.0), axis=1, keepdims=True)

            big(ROUNDS, mean_of, assign_rows)
            means_ref[...] = cent[ROUNDS % 2].reshape(K, E).astype(F32)

    for d in count_sends + row_sends + rank_sends + back_sends:
        d.wait_send()


def on_device(G, R, embeddings, labels, init_idx):
    tok, E = embeddings.shape
    K = init_idx.shape[1]
    S = 2 * tok // G
    T = min(256, S)
    N = G * S
    Z = R // 2
    Q = K // 2 // Z
    per = S // min(128, S)
    dma = pltpu.SemaphoreType.DMA
    vm = pltpu.VMEM
    assign, means = pl.pallas_call(
        functools.partial(kernel, G, R, tok, E, K, S, T),
        out_shape=(
            jax.ShapeDtypeStruct((tok, K), BF16),
            jax.ShapeDtypeStruct((K, E), F32),
        ),
        in_specs=[pl.BlockSpec(memory_space=pltpu.VMEM)] * 3,
        out_specs=[pl.BlockSpec(memory_space=pltpu.VMEM)] * 2,
        scratch_shapes=[
            vm((tok, E), BF16),
            vm((G - 1, S, E), BF16),
            vm((G, S, E), BF16),
            vm((N, K), F32),
            vm((N, K), BF16),
            vm((2, K // 2, N), BF16),
            vm((2, K // 2, E // 2), F32),
            vm((G, S, K), BF16),
            vm((tok, 1), jnp.int32),
            vm((G, 1, 128), F32),
            vm((R, 1, 128), F32),
            vm((2, R, 1, K), F32),
            vm((2, K // 2, E // 2), BF16),
            vm((2, 2, K // 2, E // 2), BF16),
            vm((2, Z, Q, E // 2), BF16),
            vm((2, 2, Z, Q, E // 2), BF16),
            vm((2, 2, Z, Q, E), BF16),
            dma(((G + 1) * per,)), dma((G * per,)),
            dma((G,)), dma((G,)),
            dma((R,)), dma((R,)),
            dma((2, R)), dma((2, R)),
            dma((2, 2)), dma((2, 2)),
            dma((2, 2, Z)), dma((2, 2, Z)),
            dma((2, Z)), dma((2, Z)),
            dma((2, Z)), dma((2, Z)),
            dma((G,)), dma((G,)),
        ],
        compiler_params=pltpu.CompilerParams(
            collective_id=0, has_side_effects=True, vmem_limit_bytes=48 * 1024 * 1024,
        ),
    )(embeddings, labels.reshape(1, tok), init_idx.reshape(K, 1))
    return (assign, means[None])


def solution(mesh):
    return jax.shard_map(
        functools.partial(on_device, mesh.shape["sc"], mesh.shape["rows"]),
        mesh=mesh,
        in_specs=(P(("sc", "rows"), None), P(("sc", "rows"), None), P("sc", None)),
        out_specs=(P(("sc", "rows"), None), P("sc", None, None)),
        check_vma=False,
    )
```
